256 devices in a mesh: pipe: 32 (over z, y), expert: 8 (over x, core).
Axes of the slice: x: 4, y: 4, z: 8, core: 2. Of those that a mesh axis runs over, the one named last changes fastest.
Arguments:
- saved: bfloat16 [2, 1024, 6144], P(None, 'expert', 'pipe'), may hold values from -6 to 6
- top_grad: bfloat16 [2, 1024, 6144], P(None, 'expert', 'pipe'), may hold values from -6 to 6
- norm_gain: float32 [6144], P('pipe'), may hold values from 0.1 to 1.9
- w_gate: bfloat16 [8, 6144, 8192], P('expert', None, 'pipe'), may hold values from -0.078125 to 0.078125
- w_up: bfloat16 [8, 6144, 8192], P('expert', None, 'pipe'), may hold values from -0.078125 to 0.078125
- w_down: bfloat16 [8, 8192, 6144], P('expert', 'pipe'), may hold values from -0.0625 to 0.0625
- routes: int32 [2, 1024, 2], P(None, 'expert'), may hold values from 0 to 7, all different within a row; in each aligned block of 128 rows (0 to 127, 128 to 255, ..., all dimensions but the last counted through in order) at most 48 rows name the same one
- gates: float32 [2, 1024, 2], P(None, 'expert'), may hold values from 0.1 to 0.9
Outputs:
- input_grads: float32 [2, 1024, 6144], P(None, 'expert', 'pipe')
- grad_gain: float32 [6144], P('pipe')
The draws below stay inside these ranges and needn't reach their ends.
Inputs may be any that keep to these rules, and one draw needn't show every extreme that they name: `routes`: each token names two different experts; in every aligned block of 128 rows of one micro-batch no expert is named more than 48 times, a bound that some block reaches.
All inputs are finite; a program needn't handle non-finite values.
Results may differ from the reference program's by a relative error of at most 0.017.
Values may be sent and summed in bfloat16 or wider, within the bound.
No kernel may reach another device: no remote copies, remote signals or barrier semaphores. Data moves between devices by JAX's collectives and lax.ppermute only.
A program may use at most 128 MiB of HBM per device.

```python
import math
import jax
import jax.numpy as jnp
import numpy as np
from jax import lax

D = 6144
EXPERTS = 8
FF = 8192
FF_DEV = 256
MB = 2
TOK_DEV = 128
TOKENS = 1024
CAP = 48
N_PIPE = 32
N_EXPERT = 8


def steps_of(stream_key, extent, shards, low, largest):
    def one(dim, shards_of):
        steps = jax.random.uniform(jax.random.fold_in(jax.random.fold_in(stream_key, 6), dim), (shards_of,), jnp.float32, low / len(shards), largest / len(shards))
        return jnp.repeat(jnp.exp(steps), extent[dim] // shards_of).reshape((-1,) + (1,) * (len(extent) - dim - 1))

    level = one(*shards[0])
    for cut in shards[1:]:
        level = level * one(*cut)
    return level


def routed_block(own_key, own, number, rows, amount, top, most, skew):
    sequence = jax.random.permutation(own_key, amount)
    packed, common = load_shares(amount, rows * top, most, skew, True), load_shares(amount, rows * top, most, skew, False)
    places = jnp.arange(amount)

    def named(sizes, offset_by):
        used = int((sizes > 0).sum())
        fixed = max(1, used // 4)
        moved = fixed + (places - fixed + offset_by * (used - fixed)) % max(1, amount - fixed)
        return jnp.zeros((amount,), jnp.int32).at[sequence[jnp.where(places < fixed, places, moved)]].set(jnp.asarray(sizes, jnp.int32))

    sizes = jnp.where(number % 4 == 0, named(packed, number // 4), named(common, number - number // 4 - 1))
    mixed = jax.random.permutation(jax.random.fold_in(own, 3), amount)
    donor, receiver = mixed[0:amount // 2 * 2:2], mixed[1:amount // 2 * 2:2]
    room = jnp.minimum(sizes[donor] - 1, most - sizes[receiver]) // 2
    room = jnp.where((donor == sequence[0]) | (receiver == sequence[0]) | (sizes[receiver] == 0), 0, jnp.maximum(room, 0))
    moved = jax.random.randint(jax.random.fold_in(own, 4), (amount // 2,), 0, 1 << 20) % (room + 1)
    sizes = sizes.at[donor].add(-moved).at[receiver].add(moved)
    items = jnp.searchsorted(jnp.cumsum(sizes), jnp.arange(rows * top), side="right").astype(jnp.int32)
    grid = items.reshape(top, rows).T
    grid = grid[jax.random.permutation(jax.random.fold_in(own, 1), rows)]
    offset_by = jax.random.randint(jax.random.fold_in(own, 2), (rows, 1), 0, top)
    return jnp.take_along_axis(grid, (jnp.arange(top)[None, :] + offset_by) % top, axis=1)


def load_shares(amount, total, bound, skew, full):
    portions = [(1 << 20) // math.isqrt(standing ** skew) + 1 for standing in range(1, amount + 1)]
    largest = bound if full else min(bound, max(-(-total // amount), total * portions[0] // sum(portions)))
    least = 1 if total - largest >= amount - 1 else 0
    holding, spare = [largest] + [least] * (amount - 1), total - largest - least * (amount - 1)
    while spare > 0:
        free = [i for i in range(1, amount) if holding[i] < largest] or [i for i in range(1, amount) if holding[i] < bound]
        whole, budget = sum([portions[i] for i in free]), spare
        for i in free:
            more = min(bound - holding[i], max(1, budget * portions[i] // whole), spare)
            holding[i] = holding[i] + more
            spare = spare - more
    return np.array(holding)


def normal_values(key, shape, scale, limit, split=(), kind=jnp.bfloat16):
    entries = jax.random.normal(key, shape, jnp.float32) * scale
    if len(split) > 0:
        entries = steps_of(key, shape, split, -0.22, 0.18) * entries
    return jnp.clip(entries, min=-limit, max=limit).astype(kind)


def setup_inputs(seed: int = 0) -> dict:
    key_of = jax.random.split(jax.random.key(seed), 9)
    saved = normal_values(key_of[0], (MB, TOKENS, D), 1.0, 6.0, ((1, 8), (2, 32)))
    top_grad = normal_values(key_of[1], (MB, TOKENS, D), 1.0, 6.0, ((1, 8), (2, 32)))
    norm_gain = jnp.clip(1.0 + 0.18 * jax.random.normal(key_of[2], (D,), jnp.float32), 0.1, 1.9)
    w_gate = normal_values(key_of[3], (EXPERTS, D, FF), D ** -0.5, 0.078125, ((0, 8), (2, 32)))
    w_up = normal_values(key_of[4], (EXPERTS, D, FF), D ** -0.5, 0.078125, ((0, 8), (2, 32)))
    w_down = normal_values(key_of[5], (EXPERTS, FF, D), FF ** -0.5, 0.0625, ((0, 8), (1, 32)))
    routes_keys = jax.random.split(jax.random.fold_in(key_of[6], 1), MB * TOKENS // TOK_DEV)
    routes_turns = jax.random.permutation(jax.random.fold_in(key_of[6], 3), MB * TOKENS // TOK_DEV)
    routes = jax.vmap(lambda own, number: routed_block(jax.random.fold_in(key_of[6], 2), own, number, TOK_DEV, EXPERTS, 2, CAP, 2))(routes_keys, routes_turns).reshape((MB, TOKENS, 2))
    gates = jnp.clip(0.1 + 0.79999997 * jax.random.uniform(key_of[7], (MB, TOKENS, 2), jnp.float32) ** steps_of(key_of[7], (MB, TOKENS, 2), ((1, 8),), -0.2, 0.2), 0.1, 0.9)
    return {"saved": saved, "top_grad": top_grad, "norm_gain": norm_gain, "w_gate": w_gate, "w_up": w_up, "w_down": w_down, "routes": routes, "gates": gates}


eps = 1e-05

def expert_rows(item):
    rows_x, rows_g, wg, wu, down_weight = item
    pre_a = jnp.dot(rows_x, wg, preferred_element_type=jnp.float32)
    pre_b = jnp.dot(rows_x, wu, preferred_element_type=jnp.float32)
    d_hidden = jnp.dot(rows_g, down_weight.T, preferred_element_type=jnp.float32)
    sig = jax.nn.sigmoid(pre_a)
    act = pre_a * sig
    d_a = (d_hidden * pre_b * sig * (1.0 + pre_a * (1.0 - sig))).astype(jnp.bfloat16)
    d_b = (d_hidden * act).astype(jnp.bfloat16)
    count = rows_x.shape[0]
    split_a = d_a.reshape(count, N_PIPE, FF_DEV).transpose(1, 0, 2)
    split_b = d_b.reshape(count, N_PIPE, FF_DEV).transpose(1, 0, 2)
    split_g = wg.reshape(D, N_PIPE, FF_DEV).transpose(1, 0, 2)
    split_u = wu.reshape(D, N_PIPE, FF_DEV).transpose(1, 0, 2)

    def add(total, group):
        part_a, part_b, part_g, part_u = group
        partial_value = jnp.dot(part_a, part_g.T, preferred_element_type=jnp.float32)
        partial_value = partial_value + jnp.dot(part_b, part_u.T, preferred_element_type=jnp.float32)
        partial_value = lax.optimization_barrier(partial_value.astype(jnp.bfloat16)).astype(jnp.float32)
        return (total + partial_value, None)
    total, unused = lax.scan(add, jnp.zeros((count, D), jnp.float32), (split_a, split_b, split_g, split_u))
    return total.astype(jnp.bfloat16)

def reference(saved, top_grad, norm_gain, w_gate, w_up, w_down, routes, gates):
    grads = []
    gain_total = jnp.zeros((D,), jnp.float32)
    for batch in range(MB):
        xf = saved[batch].astype(jnp.float32)
        dy = top_grad[batch].astype(jnp.float32)
        scale = lax.rsqrt(lax.optimization_barrier(jnp.mean(xf * xf, axis=-1, keepdims=True)) + eps)
        normed = (xf * scale * norm_gain).astype(jnp.bfloat16)
        blocks = routes[batch].reshape(N_EXPERT, 2 * TOK_DEV)
        onehot = (blocks[:, :, None] == jnp.arange(EXPERTS, dtype=jnp.int32)[None, None, :]).astype(jnp.int32)
        before = jnp.cumsum(onehot, axis=1) - onehot
        slot = lax.optimization_barrier(jnp.sum(before * onehot, axis=-1)).astype(jnp.int32)
        source = jnp.arange(N_EXPERT, dtype=jnp.int32)[:, None]
        target = (blocks * (N_EXPERT * CAP) + source * CAP + slot).reshape(-1).astype(jnp.int32)
        pairs = jnp.repeat(normed, 2, axis=0)
        rows_x = jnp.zeros((EXPERTS * N_EXPERT * CAP, D), normed.dtype).at[target].set(pairs)
        pair_grad = (gates[batch][:, :, None] * dy[:, None, :]).reshape(2 * TOKENS, D).astype(jnp.bfloat16)
        rows_g = jnp.zeros((EXPERTS * N_EXPERT * CAP, D), pair_grad.dtype).at[target].set(pair_grad)
        d_rows = lax.map(expert_rows, (rows_x.reshape(EXPERTS, N_EXPERT * CAP, D), rows_g.reshape(EXPERTS, N_EXPERT * CAP, D), w_gate, w_up, w_down))
        d_pairs = d_rows.reshape(EXPERTS * N_EXPERT * CAP, D)[target].astype(jnp.float32)
        d_norm = d_pairs.reshape(TOKENS, 2, D).sum(axis=1)
        gain_total = gain_total + lax.optimization_barrier(jnp.sum(d_norm * xf * scale, axis=0))
        scaled = norm_gain * d_norm
        d_x = scale * scaled - xf * scale ** 3 * lax.optimization_barrier(jnp.mean(scaled * xf, axis=-1, keepdims=True))
        grads.append(dy + d_x)
    return (jnp.stack(grads), gain_total)
```

```python
import jax
import jax.numpy as jnp
from jax import lax
from jax.experimental import pallas as pl
from jax.experimental.pallas import tpu as pltpu
from jax.sharding import Mesh
from jax.sharding import PartitionSpec as P

PIPE = ("pipe_0", "pipe_1")
EPS = 1e-05
F32 = jnp.float32
BF16 = jnp.bfloat16


def send(x, axis, to):
    n = lax.axis_size(axis)
    return lax.ppermute(x, axis, [(i, to(i) % n) for i in range(n)])


def from_offset(x, axis, d):
    return send(x, axis, lambda i: i - d)


def gather_ring(x, axis):
    n, rows = lax.axis_size(axis), x.shape[0]
    half = rows // 2
    ahead, behind, out = x, x, [(0, 0, rows, x)]
    for s in range(1, n // 2):
        ahead = from_offset(ahead, axis, 1)
        behind = from_offset(behind, axis, -1)
        out += [(s, 0, rows, ahead), (n - s, 0, rows, behind)]
    out.append((n // 2, 0, half, from_offset(ahead[:half], axis, 1)))
    out.append((n // 2, half, rows, from_offset(behind[half:], axis, -1)))
    return out


def in_order(pieces):
    return jnp.concatenate([p[3] for p in sorted(pieces, key=lambda p: (p[0], p[1]))], axis=0)


def scatter_ring(term, rows, axis):
    n = lax.axis_size(axis)
    half, far = rows // 2, n // 2
    up = term(far, 0, half).astype(BF16)
    down = term(far, half, rows).astype(BF16)
    for s in range(far - 1, 0, -1):
        got_up = from_offset(up, axis, -1).astype(F32)
        got_down = from_offset(down, axis, 1).astype(F32)
        if s == far - 1:
            up = jnp.concatenate(
                [(term(s, 0, half) + got_up).astype(BF16), term(s, half, rows).astype(BF16)], axis=0
            )
            down = jnp.concatenate(
                [term(n - s, 0, half).astype(BF16), (term(n - s, half, rows) + got_down).astype(BF16)],
                axis=0,
            )
        else:
            up = (term(s, 0, rows) + got_up).astype(BF16)
            down = (term(n - s, 0, rows) + got_down).astype(BF16)
    got_up = from_offset(up, axis, -1).astype(F32)
    got_down = from_offset(down, axis, 1).astype(F32)
    return term(0, 0, rows) + got_up + got_down


def sum_ring(x, axis):
    d = lax.axis_size(axis) // 2
    while d:
        x = x + from_offset(x, axis, d)
        d //= 2
    return x


def thirds(x):
    high = lax.reduce_precision(x, 8, 7)
    rest = x - high
    middle = lax.reduce_precision(rest, 8, 7)
    return [high.astype(BF16), middle.astype(BF16), (rest - middle).astype(BF16)]


def expert_gather(x):
    half = x.shape[0] // 2
    behind = send(x, "expert", lambda i: i + 2)
    ahead = send(x, "expert", lambda i: i - 2)
    far = jnp.concatenate(
        [send(behind[:half], "expert", lambda i: i + 2), send(ahead[half:], "expert", lambda i: i - 2)],
        axis=0,
    )
    mine = jnp.concatenate([x, behind, ahead, far], axis=1)
    return jnp.concatenate([mine, send(mine, "expert", lambda i: i ^ 1)], axis=1)


def expert_return(x):
    block = x.shape[1] // 8
    other = send(x[:, 4 * block :], "expert", lambda i: i ^ 1)
    mine = (x[:, : 4 * block].astype(F32) + other.astype(F32)).astype(x.dtype)
    a = send(mine[:, block : 2 * block], "expert", lambda i: i - 2)
    b = send(mine[:, 2 * block : 3 * block], "expert", lambda i: i + 2)
    c = send(mine[:, 3 * block :], "expert", lambda i: i + 4)
    return mine[:, :block].astype(F32) + a.astype(F32) + b.astype(F32) + c.astype(F32)


def sum_expert(x):
    x = x + send(x, "expert", lambda i: i ^ 1)
    x = x + send(x, "expert", lambda i: i + 4)
    return x + send(x, "expert", lambda i: i + 2)


def contract(a, b, da, db):
    return lax.dot_general(a, b, (((da,), (db,)), ((), ())), preferred_element_type=F32)


def order_kernel(pos, wg, wu, wd, in_a, in_b, down_a, down_b, turned):
    n_y, part, hidden = wg.shape[1:]
    turned[...] = wd[...].T.reshape(n_y, part, hidden)
    for dy in range(n_y):
        at = lax.rem(pos[1] + dy, n_y)
        gate, up, down = wg[0, at], wu[0, at], turned[at]
        in_a[0, dy, :, :hidden] = gate
        in_a[0, dy, :, hidden:] = up
        in_b[dy, 0, :, :hidden] = gate
        in_b[dy, 0, :, hidden:] = up
        down_a[0, dy] = down
        down_b[dy, 0] = down


def ordered_weights(pos, wg, wu, wd, n_z, n_y):
    width, hidden = wg.shape
    part = width // (n_z * n_y)

    def at(i, pos):
        return lax.rem(pos[0] + i, n_z)

    def both(cols):
        return [
            pl.BlockSpec((1, n_y, part, cols), lambda i, pos: (i, 0, 0, 0)),
            pl.BlockSpec((n_y, 1, part, cols), lambda i, pos: (0, i, 0, 0)),
        ]

    def shapes(cols):
        return [
            jax.ShapeDtypeStruct((n_z, n_y, part, cols), BF16),
            jax.ShapeDtypeStruct((n_y, n_z, part, cols), BF16),
        ]

    spec = pl.BlockSpec((1, n_y, part, hidden), lambda i, pos: (at(i, pos), 0, 0, 0))
    out = pl.pallas_call(
        order_kernel,
        grid_spec=pltpu.PrefetchScalarGridSpec(
            num_scalar_prefetch=1,
            grid=(n_z,),
            in_specs=[
                spec,
                spec,
                pl.BlockSpec((hidden, n_y * part), lambda i, pos: (0, at(i, pos))),
            ],
            out_specs=both(2 * hidden) + both(hidden),
            scratch_shapes=[pltpu.VMEM((n_y, part, hidden), BF16)],
        ),
        out_shape=shapes(2 * hidden) + shapes(hidden),
        cost_estimate=pl.CostEstimate(
            flops=0, bytes_accessed=18 * width * hidden, transcendentals=0
        ),
    )(
        pos,
        wg.reshape(n_z, n_y, part, hidden),
        wu.reshape(n_z, n_y, part, hidden),
        wd,
    )
    return [o.reshape(width, -1) for o in out]


def body(saved, top_grad, norm_gain, w_gate, w_up, w_down, routes, gates):
    n_z, n_y = lax.axis_size(PIPE[0]), lax.axis_size(PIPE[1])
    n_experts = lax.axis_size("expert")
    micro, tok, part = saved.shape
    width = part * n_z * n_y
    hidden = w_gate.shape[2]
    cap = 3 * tok // n_experts
    rows = n_experts * cap
    me = lax.axis_index("expert").astype(F32)
    gain = norm_gain[:, None]
    x_t = jnp.swapaxes(saved, 1, 2)
    dy_t = jnp.swapaxes(top_grad, 1, 2)

    names = jnp.swapaxes(routes, 1, 2)
    ids = jnp.arange(n_experts, dtype=jnp.int32)
    hits = (names[:, :, None, :] == ids[None, None, :, None]).astype(F32)
    count = jnp.sum(hits, axis=1)
    lane = jnp.arange(tok, dtype=jnp.int32)
    earlier = (lane[:, None] < lane[None, :]).astype(BF16)
    before = lax.dot_general(
        count.astype(BF16).reshape(micro * n_experts, tok),
        earlier,
        (((1,), (0,)), ((), ())),
        preferred_element_type=F32,
    ).reshape(micro, 1, n_experts, tok)
    slots = jnp.sum(hits * before, axis=2)
    weights = jnp.swapaxes(gates, 1, 2)
    facts = jnp.concatenate(
        [names.astype(BF16), slots.astype(BF16)] + thirds(weights) + [jnp.zeros((micro, 6, tok), BF16)],
        axis=1,
    )
    payload = jnp.concatenate([x_t, dy_t, facts], axis=1)

    column = jnp.arange(n_experts * tok, dtype=jnp.int32)[None, :]
    first_row = (column // tok * cap).astype(F32)
    row = jnp.arange(rows, dtype=jnp.int32)[:, None].astype(F32)
    placing, saved_rows, blocks, gate_rows, squares = [], [], [], [], []
    for m in range(micro):
        everyone = expert_gather(payload[m])
        fact = everyone[2 * part :].astype(F32)
        own = [fact[k : k + 1] == me for k in range(2)]
        at = [jnp.where(own[k], first_row + fact[2 + k : 3 + k], -1.0) for k in range(2)]
        place = ((row == at[0]) | (row == at[1])).astype(BF16)
        pieces = jnp.concatenate(
            [
                jnp.where(own[0], fact[4 + 2 * k : 5 + 2 * k], 0.0)
                + jnp.where(own[1], fact[5 + 2 * k : 6 + 2 * k], 0.0)
                for k in range(3)
            ],
            axis=0,
        ).astype(BF16)
        taken = contract(everyone[: 2 * part], place, 1, 1)
        x_rows = taken[:part]
        placing.append(place)
        saved_rows.append(x_rows.astype(BF16))
        gate_rows.append(jnp.sum(contract(pieces, place, 1, 1), axis=0, keepdims=True))
        blocks.append(jnp.concatenate([(x_rows * gain).astype(BF16), taken[part:].astype(BF16)], axis=1))
        tokens = everyone[:part].astype(F32)
        squares.append(jnp.sum(tokens * tokens, axis=0, keepdims=True))

    pos = jnp.stack([lax.axis_index(PIPE[0]), lax.axis_index(PIPE[1])]).astype(jnp.int32)
    pos, first_block = lax.optimization_barrier((pos, blocks[0]))
    in_a, in_b, down_a, down_b = ordered_weights(pos, w_gate[0], w_up[0], w_down[0], n_z, n_y)

    got_a = gather_ring(in_order(gather_ring(first_block, PIPE[1])), PIPE[0])
    got_b = gather_ring(in_order(gather_ring(blocks[1], PIPE[0])), PIPE[1])

    total = sum_ring(sum_ring(jnp.concatenate(squares, axis=0), PIPE[1]), PIPE[0])
    scale = lax.rsqrt(total / width + EPS)

    def hidden_sums(got, w_in, w_out, span):
        pre, back = None, None
        for off, lo, hi, x in got:
            a, b = off * span + lo, off * span + hi
            p = contract(w_in[a:b], x[:, :rows], 0, 0)
            d = contract(w_out[a:b], x[:, rows:], 0, 0)
            pre = p if pre is None else pre + p
            back = d if back is None else back + d
        return pre, back

    d_hidden, inner_rows, scale_rows = [], [], []
    for m, (got, w_in, w_out, span) in enumerate(
        [(got_a, in_a, down_a, n_y * part), (got_b, in_b, down_b, n_z * part)]
    ):
        pre, back = hidden_sums(got, w_in, w_out, span)
        pieces = jnp.concatenate(thirds(scale[m : m + 1]), axis=0)
        scale_row = jnp.sum(contract(pieces, placing[m], 1, 1), axis=0, keepdims=True)
        pre_a, pre_b = pre[:hidden] * scale_row, pre[hidden:] * scale_row
        back = back * gate_rows[m]
        sig = jax.nn.sigmoid(pre_a)
        d_a = back * pre_b * sig * (1.0 + pre_a * (1.0 - sig))
        d_b = back * pre_a * sig
        inner_rows.append(jnp.sum(d_a * pre[:hidden] + d_b * pre[hidden:], axis=0, keepdims=True))
        scale_rows.append(scale_row)
        d_hidden.append(jnp.concatenate([d_a, d_b], axis=0).astype(BF16))

    def terms(w_in, d, span):
        return lambda off, lo, hi: contract(w_in[off * span + lo : off * span + hi], d, 1, 0)

    def parts(x):
        return lambda off, lo, hi: x[off * part + lo : off * part + hi]

    near_a = scatter_ring(terms(in_a, d_hidden[0], n_y * part), n_y * part, PIPE[0])
    near_b = scatter_ring(terms(in_b, d_hidden[1], n_z * part), n_z * part, PIPE[1])
    d_rows = [
        scatter_ring(parts(near_a), part, PIPE[1]).astype(BF16),
        scatter_ring(parts(near_b), part, PIPE[0]).astype(BF16),
    ]

    inner_rows = sum_ring(sum_ring(jnp.concatenate(inner_rows, axis=0), PIPE[1]), PIPE[0])
    inner = []
    for m in range(micro):
        pieces = jnp.concatenate(thirds(inner_rows[m : m + 1]), axis=0)
        inner.append(jnp.sum(contract(pieces, placing[m], 1, 0), axis=0, keepdims=True))
    inner = expert_return(jnp.concatenate(inner, axis=0)) / width

    grads, gain_part = [], 0.0
    for m in range(micro):
        d_tokens = contract(d_rows[m], placing[m], 1, 0).astype(BF16)
        d_norm = expert_return(d_tokens)
        gain_part = gain_part + jnp.sum(
            d_rows[m].astype(F32) * saved_rows[m].astype(F32) * scale_rows[m], axis=1
        )
        own = scale[m : m + 1, :tok]
        d_x = own * gain * d_norm - x_t[m].astype(F32) * (own * own * own * inner[m : m + 1])
        grads.append(dy_t[m].astype(F32) + d_x)
    input_grads = jnp.swapaxes(jnp.stack(grads), 1, 2)
    return input_grads, sum_expert(gain_part)


def solution(mesh):
    torus = Mesh(mesh.devices.reshape(8, 4, mesh.shape["expert"]), (*PIPE, "expert"))
    in_specs = (
        P(None, "expert", PIPE),
        P(None, "expert", PIPE),
        P(PIPE),
        P("expert", None, PIPE),
        P("expert", None, PIPE),
        P("expert", PIPE, None),
        P(None, "expert", None),
        P(None, "expert", None),
    )
    out_specs = (P(None, "expert", PIPE), P(PIPE))
    return jax.shard_map(body, mesh=torus, in_specs=in_specs, out_specs=out_specs, check_vma=False)
```

```python
import functools

import jax
import jax.numpy as jnp
from jax import lax
from jax.experimental import pallas as pl
from jax.experimental.pallas import tpu as pltpu
from jax.sharding import Mesh
from jax.sharding import PartitionSpec as P

PIPE = ("pipe_0", "pipe_1")
EPS = 1e-05
F32 = jnp.float32
BF16 = jnp.bfloat16


def send(x, axis, to):
    n = lax.axis_size(axis)
    return lax.ppermute(x, axis, [(i, to(i) % n) for i in range(n)])


def from_offset(x, axis, d):
    return send(x, axis, lambda i: i - d)


def arrival(n):
    out = [0]
    for s in range(1, n // 2):
        out += [s, n - s]
    return out + [n // 2]


def gather_ring(x, axis, beside=None):
    n, half = lax.axis_size(axis), x.shape[0] // 16 * 8
    ahead, behind, out = x, x, [x]
    for s in range(1, n // 2):
        ahead = from_offset(ahead, axis, 1)
        behind = from_offset(behind, axis, -1)
        if s == 1 and beside is not None:
            ahead, behind, beside = lax.optimization_barrier((ahead, behind, beside))
        out += [ahead, behind]
    last = [from_offset(ahead[:half], axis, 1), from_offset(behind[half:], axis, -1)]
    return out + [last], beside


def whole(piece):
    return jnp.concatenate(piece, axis=0) if isinstance(piece, list) else piece


def scatter_ring(term, rows, axis, beside=None, steps=()):
    n = lax.axis_size(axis)
    half, far = rows // 2, n // 2
    up = term(far, 0, half).astype(BF16)
    down = term(far, half, rows).astype(BF16)
    steps = list(steps)
    for s in range(far - 1, -1, -1):
        got_up = from_offset(up, axis, -1)
        got_down = from_offset(down, axis, 1)
        if steps:
            other, d = steps.pop(0)
            got_up, got_down, beside = lax.optimization_barrier((got_up, got_down, beside))
            beside = beside + from_offset(beside, other, d)
        if s == far - 1:
            got_up = jnp.pad(got_up, ((0, rows - half), (0, 0)))
            got_down = jnp.pad(got_down, ((half, 0), (0, 0)))
        if s > 0:
            up = (term(s, 0, rows) + got_up.astype(F32)).astype(BF16)
            down = (term(n - s, 0, rows) + got_down.astype(F32)).astype(BF16)
    return term(0, 0, rows) + got_up.astype(F32) + got_down.astype(F32), beside


def sum_pipe(x):
    n = lax.axis_size(PIPE)
    every = jnp.broadcast_to(x[None], (n, *x.shape))
    return jnp.sum(lax.all_to_all(every, PIPE, 0, 0, tiled=True), axis=0)


def thirds(x):
    high = lax.reduce_precision(x, 8, 7)
    rest = x - high
    middle = lax.reduce_precision(rest, 8, 7)
    return [high.astype(BF16), middle.astype(BF16), (rest - middle).astype(BF16)]


def expert_gather(x):
    half = x.shape[0] // 2
    behind = send(x, "expert", lambda i: i + 2)
    ahead = send(x, "expert", lambda i: i - 2)
    far = jnp.concatenate(
        [send(behind[:half], "expert", lambda i: i + 2), send(ahead[half:], "expert", lambda i: i - 2)],
        axis=0,
    )
    mine = jnp.concatenate([x, behind, ahead, far], axis=2)
    return jnp.concatenate([mine, send(mine, "expert", lambda i: i ^ 1)], axis=2)


def expert_return(x, extras):
    def packed(x, extras):
        rows = [p for e in extras for p in thirds(e)]
        pad = jnp.zeros((x.shape[0], 8 - len(rows), x.shape[2]), BF16)
        return jnp.concatenate([x.astype(BF16)] + rows + [pad], axis=1)

    def rows_of(x):
        r = x.shape[1] - 8
        return x[:, :r].astype(F32), [
            jnp.sum(x[:, r + 3 * k : r + 3 * k + 3].astype(F32), axis=1, keepdims=True)
            for k in range(len(extras))
        ]

    def plus(a, b):
        return a[0] + b[0], [p + q for p, q in zip(a[1], b[1])]

    all_ = packed(x, extras)
    block = x.shape[2] // 8
    other = send(all_[:, :, 4 * block :], "expert", lambda i: i ^ 1)
    mine = plus(rows_of(all_[:, :, : 4 * block]), rows_of(other))
    mine = packed(*mine)
    behind = rows_of(send(mine[:, :, block : 2 * block], "expert", lambda i: i - 2))
    ahead = rows_of(send(mine[:, :, 2 * block : 3 * block], "expert", lambda i: i + 2))
    far = rows_of(send(mine[:, :, 3 * block :], "expert", lambda i: i + 4))
    return plus(plus(rows_of(mine[:, :, :block]), far), plus(behind, ahead))


def contract(a, b, da, db):
    return lax.dot_general(a, b, (((da,), (db,)), ((), ())), preferred_element_type=F32)


def order_kernel(order, places, y, wg, wu, wd, in_a, in_b, down_a, down_b, turned):
    n_y, part, hidden = wg.shape[1:]
    turned[...] = wd[...].T.reshape(n_y, part, hidden)
    for j, dy in enumerate(order):
        at = lax.rem(y[0] + dy, n_y)
        gate, up, down = wg[0, at], wu[0, at], turned[at]
        in_a[0, j, :, :hidden] = gate
        in_a[0, j, :, hidden:] = up
        in_b[j, 0, :, :hidden] = gate
        in_b[j, 0, :, hidden:] = up
        down_a[0, j] = down
        down_b[j, 0] = down


def ordered_weights(z, y, wg, wu, wd, n_z, n_y):
    width, hidden = wg.shape
    part = width // (n_z * n_y)
    places = lax.rem(z + jnp.array(arrival(n_z), jnp.int32), n_z)

    def both(cols):
        return [
            pl.BlockSpec((1, n_y, part, cols), lambda i, p, y: (i, 0, 0, 0)),
            pl.BlockSpec((n_y, 1, part, cols), lambda i, p, y: (0, i, 0, 0)),
        ]

    def shapes(cols):
        return [
            jax.ShapeDtypeStruct((n_z, n_y, part, cols), BF16),
            jax.ShapeDtypeStruct((n_y, n_z, part, cols), BF16),
        ]

    spec = pl.BlockSpec((1, n_y, part, hidden), lambda i, p, y: (p[i], 0, 0, 0))
    out = pl.pallas_call(
        functools.partial(order_kernel, arrival(n_y)),
        grid_spec=pltpu.PrefetchScalarGridSpec(
            num_scalar_prefetch=2,
            grid=(n_z,),
            in_specs=[
                spec,
                spec,
                pl.BlockSpec((hidden, n_y * part), lambda i, p, y: (0, p[i])),
            ],
            out_specs=both(2 * hidden) + both(hidden),
            scratch_shapes=[pltpu.VMEM((n_y, part, hidden), BF16)],
        ),
        out_shape=shapes(2 * hidden) + shapes(hidden),
        cost_estimate=pl.CostEstimate(
            flops=0, bytes_accessed=18 * width * hidden, transcendentals=0
        ),
    )(
        places,
        y[None],
        wg.reshape(n_z, n_y, part, hidden),
        wu.reshape(n_z, n_y, part, hidden),
        wd,
    )
    return [o.reshape(width, -1) for o in out]


def batched(a, b, da, db):
    return lax.dot_general(a, b, (((da,), (db,)), ((0,), (0,))), preferred_element_type=F32)


def body(saved, top_grad, norm_gain, w_gate, w_up, w_down, routes, gates):
    n_z, n_y = lax.axis_size(PIPE[0]), lax.axis_size(PIPE[1])
    n_experts = lax.axis_size("expert")
    micro, tok, part = saved.shape
    width = part * n_z * n_y
    hidden = w_gate.shape[2]
    cap = 3 * tok // n_experts
    rows = n_experts * cap
    me = lax.axis_index("expert").astype(F32)
    gain = norm_gain[:, None]
    x_t = jnp.swapaxes(saved, 1, 2)
    dy_t = jnp.swapaxes(top_grad, 1, 2)
    own_x = x_t.astype(F32)

    names = jnp.swapaxes(routes, 1, 2)
    ids = jnp.arange(n_experts, dtype=jnp.int32)
    hits = (names[:, :, None, :] == ids[None, None, :, None]).astype(F32)
    count = jnp.sum(hits, axis=1)
    lane = jnp.arange(tok, dtype=jnp.int32)
    earlier = (lane[:, None] < lane[None, :]).astype(BF16)
    before = contract(
        count.astype(BF16).reshape(micro * n_experts, tok), earlier, 1, 0
    ).reshape(micro, 1, n_experts, tok)
    slots = jnp.sum(hits * before, axis=2)
    weights = jnp.swapaxes(gates, 1, 2)
    facts = jnp.concatenate(
        [names.astype(BF16), slots.astype(BF16)] + thirds(weights) + [jnp.zeros((micro, 6, tok), BF16)],
        axis=1,
    )
    everyone = expert_gather(jnp.concatenate([x_t, dy_t, facts], axis=1))

    column = jnp.arange(n_experts * tok, dtype=jnp.int32)[None, None, :]
    first_row = (column // tok * cap).astype(F32)
    row = jnp.arange(rows, dtype=jnp.int32)[None, :, None].astype(F32)
    fact = everyone[:, 2 * part :].astype(F32)
    own = [fact[:, k : k + 1] == me for k in range(2)]
    at = [jnp.where(own[k], first_row + fact[:, 2 + k : 3 + k], -1.0) for k in range(2)]
    placing = ((row == at[0]) | (row == at[1])).astype(BF16)
    pieces = jnp.concatenate(
        [
            jnp.where(own[0], fact[:, 4 + 2 * k : 5 + 2 * k], 0.0)
            + jnp.where(own[1], fact[:, 5 + 2 * k : 6 + 2 * k], 0.0)
            for k in range(3)
        ],
        axis=1,
    ).astype(BF16)
    taken = batched(everyone[:, : 2 * part], placing, 2, 2)
    x_rows = taken[:, :part]
    saved_rows = x_rows.astype(BF16)
    blocks = jnp.concatenate(
        [(x_rows * gain).astype(BF16), taken[:, part:].astype(BF16)], axis=2
    )
    gate_rows = jnp.sum(batched(pieces, placing, 2, 2), axis=1, keepdims=True)

    line_a = jnp.concatenate([whole(p) for p in gather_ring(blocks[0], PIPE[1])[0]], axis=0)
    line_b = jnp.concatenate([whole(p) for p in gather_ring(blocks[1], PIPE[0])[0]], axis=0)
    squares = jnp.concatenate(
        [jnp.sum(x_rows * x_rows, axis=1), jnp.sum(own_x * own_x, axis=1)], axis=1
    )
    line_a, line_b, z, y = lax.optimization_barrier(
        (line_a, line_b, lax.axis_index(PIPE[0]), lax.axis_index(PIPE[1]))
    )
    got_a, squares = gather_ring(line_a, PIPE[0], squares)
    got_b, _ = gather_ring(line_b, PIPE[1])
    in_a, in_b, down_a, down_b = ordered_weights(z, y, w_gate[0], w_up[0], w_down[0], n_z, n_y)
    scale = lax.rsqrt(sum_pipe(squares) / width + EPS)[:, None, :]
    scale_rows, scale = scale[:, :, :rows], scale[:, :, rows:]

    def hidden_sums(got, w_in, w_out):
        pre = back = None
        at = 0
        for piece in got:
            for x in piece if isinstance(piece, list) else [piece]:
                end = at + x.shape[0]
                p = contract(w_in[at:end], x[:, :rows], 0, 0)
                d = contract(w_out[at:end], x[:, rows:], 0, 0)
                pre = p if pre is None else pre + p
                back = d if back is None else back + d
                at = end
        return pre, back

    def activations(m, pre, back):
        pre_a, pre_b = pre[:hidden] * scale_rows[m], pre[hidden:] * scale_rows[m]
        back = back * gate_rows[m]
        sig = jax.nn.sigmoid(pre_a)
        d_a = back * pre_b * sig * (1.0 + pre_a * (1.0 - sig))
        d_b = back * pre_a * sig
        inner = jnp.sum(d_a * pre[:hidden] + d_b * pre[hidden:], axis=0, keepdims=True)
        return jnp.concatenate([d_a, d_b], axis=0).astype(BF16), inner

    def terms(w_in, d, span, n):
        order = arrival(n)

        def term(off, lo, hi):
            at = order.index(off) * span
            return contract(w_in[at + lo : at + hi], d, 1, 0)

        return term

    def parts(x, n):
        order = arrival(n)

        def term(off, lo, hi):
            at = order.index(off) * part
            return x[at + lo : at + hi]

        return term

    span_a, span_b = n_y * part, n_z * part
    d_b, inner_b = activations(1, *hidden_sums(got_b, in_b, down_b))
    d_a, inner_a = activations(0, *hidden_sums(got_a, in_a, down_a))
    inner = jnp.concatenate([inner_a, inner_b], axis=0)
    steps = [(PIPE[1], 2), (PIPE[1], 1), (PIPE[0], 4), (PIPE[0], 2), (PIPE[0], 1)]
    near_a, inner = scatter_ring(
        terms(in_a, d_a, span_a, n_z), span_a, PIPE[0], inner, steps[:4]
    )
    near_b, _ = scatter_ring(terms(in_b, d_b, span_b, n_y), span_b, PIPE[1])
    rows_a, inner = scatter_ring(parts(near_a, n_y), part, PIPE[1], inner, steps[4:])
    rows_b, _ = scatter_ring(parts(near_b, n_z), part, PIPE[0])
    d_rows = jnp.stack([rows_a, rows_b]).astype(BF16)

    inner = jnp.stack(thirds(inner), axis=1)
    inner = jnp.sum(batched(inner, placing, 2, 1), axis=1, keepdims=True)
    gain_part = jnp.sum(
        d_rows.astype(F32) * saved_rows.astype(F32) * scale_rows, axis=(0, 2)
    )
    gain_part = jnp.concatenate([gain_part, jnp.zeros((micro * tok - part,), F32)])
    gain_part = jnp.tile(gain_part.reshape(micro, 1, tok), (1, 1, n_experts))
    d_norm, (inner, gain_sum) = expert_return(batched(d_rows, placing, 2, 1), [inner, gain_part])
    d_x = scale * gain * d_norm - own_x * (scale * scale * scale * (inner / width))
    input_grads = jnp.swapaxes(dy_t.astype(F32) + d_x, 1, 2)
    return input_grads, gain_sum.reshape(-1)[:part]


def solution(mesh):
    torus = Mesh(mesh.devices.reshape(8, 4, mesh.shape["expert"]), (*PIPE, "expert"))
    in_specs = (
        P(None, "expert", PIPE),
        P(None, "expert", PIPE),
        P(PIPE),
        P("expert", None, PIPE),
        P("expert", None, PIPE),
        P("expert", PIPE, None),
        P(None, "expert", None),
        P(None, "expert", None),
    )
    out_specs = (P(None, "expert", PIPE), P(PIPE))
    return jax.shard_map(body, mesh=torus, in_specs=in_specs, out_specs=out_specs, check_vma=False)
```

```python
import functools

import jax
import jax.numpy as jnp
from jax import lax
from jax.experimental import pallas as pl
from jax.experimental.pallas import tpu as pltpu
from jax.sharding import Mesh
from jax.sharding import PartitionSpec as P

PIPE = ("pipe_0", "pipe_1")
EPS = 1e-05
F32 = jnp.float32
BF16 = jnp.bfloat16


def send(x, axis, to):
    n = lax.axis_size(axis)
    return lax.ppermute(x, axis, [(i, to(i) % n) for i in range(n)])


def from_offset(x, axis, d):
    return send(x, axis, lambda i: i - d)


def arrival(n):
    out = [0]
    for s in range(1, n // 2):
        out += [s, n - s]
    return out + [n // 2]


def hop(ahead, behind, axis):
    return from_offset(ahead, axis, 1), from_offset(behind, axis, -1)


def last_hop(ahead, behind, axis):
    half = ahead.shape[0] // 2
    return [from_offset(ahead[:half], axis, 1), from_offset(behind[half:], axis, -1)]


def gather_ring(x, axis):
    ahead, behind, out = x, x, [x]
    for _ in range(1, lax.axis_size(axis) // 2):
        ahead, behind = hop(ahead, behind, axis)
        out += [ahead, behind]
    return jnp.concatenate(out + last_hop(ahead, behind, axis), axis=0)


def add_from(*places):
    def step(x):
        for axis, d in places:
            x = x + from_offset(x, axis, d)
        return x

    return step


def scatter_ring(term, rows, axis, beside=None, steps=()):
    n = lax.axis_size(axis)
    half, far = rows // 2, n // 2
    up = term(far, 0, half).astype(BF16)
    down = term(far, half, rows).astype(BF16)
    steps = list(steps)
    for s in range(far - 1, -1, -1):
        got_up = from_offset(up, axis, -1)
        got_down = from_offset(down, axis, 1)
        if steps:
            other, d = steps.pop(0)
            got_up, got_down, beside = lax.optimization_barrier((got_up, got_down, beside))
            beside = beside + from_offset(beside, other, d)
        if s == far - 1:
            got_up = jnp.pad(got_up, ((0, rows - half), (0, 0)))
            got_down = jnp.pad(got_down, ((half, 0), (0, 0)))
        if s > 0:
            up = (term(s, 0, rows) + got_up.astype(F32)).astype(BF16)
            down = (term(n - s, 0, rows) + got_down.astype(F32)).astype(BF16)
    return term(0, 0, rows) + got_up.astype(F32) + got_down.astype(F32), beside


def thirds(x):
    high = lax.reduce_precision(x, 8, 7)
    rest = x - high
    middle = lax.reduce_precision(rest, 8, 7)
    return [high.astype(BF16), middle.astype(BF16), (rest - middle).astype(BF16)]


def expert_gather(x):
    half = x.shape[0] // 2
    behind = send(x, "expert", lambda i: i + 2)
    ahead = send(x, "expert", lambda i: i - 2)
    far = jnp.concatenate(
        [send(behind[:half], "expert", lambda i: i + 2), send(ahead[half:], "expert", lambda i: i - 2)],
        axis=0,
    )
    mine = jnp.concatenate([x, behind, ahead, far], axis=2)
    return jnp.concatenate([mine, send(mine, "expert", lambda i: i ^ 1)], axis=2)


def expert_return(x, extras):
    def packed(x, extras):
        rows = [p for e in extras for p in thirds(e)]
        pad = jnp.zeros((x.shape[0], 8 - len(rows), x.shape[2]), BF16)
        return jnp.concatenate([x.astype(BF16)] + rows + [pad], axis=1)

    def rows_of(x):
        r = x.shape[1] - 8
        return x[:, :r].astype(F32), [
            jnp.sum(x[:, r + 3 * k : r + 3 * k + 3].astype(F32), axis=1, keepdims=True)
            for k in range(len(extras))
        ]

    def plus(a, b):
        return a[0] + b[0], [p + q for p, q in zip(a[1], b[1])]

    all_ = packed(x, extras)
    block = x.shape[2] // 8
    other = send(all_[:, :, 4 * block :], "expert", lambda i: i ^ 1)
    mine = plus(rows_of(all_[:, :, : 4 * block]), rows_of(other))
    mine = packed(*mine)
    behind = rows_of(send(mine[:, :, block : 2 * block], "expert", lambda i: i - 2))
    ahead = rows_of(send(mine[:, :, 2 * block : 3 * block], "expert", lambda i: i + 2))
    far = rows_of(send(mine[:, :, 3 * block :], "expert", lambda i: i + 4))
    return plus(plus(rows_of(mine[:, :, :block]), far), plus(behind, ahead))


def contract(a, b, da, db):
    return lax.dot_general(a, b, (((da,), (db,)), ((), ())), preferred_element_type=F32)


def order_kernel(order, y_first, places, y, wg, wu, wd, into, down, turned):
    n_y, part, hidden = wg.shape[1:]
    turned[...] = wd[...].T.reshape(n_y, part, hidden)
    for j, dy in enumerate(order):
        at = lax.rem(y[0] + dy, n_y)
        to = (j, 0) if y_first else (0, j)
        into[*to, :, :hidden] = wg[0, at]
        into[*to, :, hidden:] = wu[0, at]
        down[*to] = turned[at]


def ordered_weights(place, wg, wu, wd, n_z, n_y, y_first):
    z, y = place
    width, hidden = wg.shape
    part = width // (n_z * n_y)
    places = lax.rem(z + jnp.array(arrival(n_z), jnp.int32), n_z)

    def out(cols):
        if y_first:
            return (
                pl.BlockSpec((n_y, 1, part, cols), lambda i, p, y: (0, i, 0, 0)),
                jax.ShapeDtypeStruct((n_y, n_z, part, cols), BF16),
            )
        return (
            pl.BlockSpec((1, n_y, part, cols), lambda i, p, y: (i, 0, 0, 0)),
            jax.ShapeDtypeStruct((n_z, n_y, part, cols), BF16),
        )

    outs = [out(2 * hidden), out(hidden)]
    spec = pl.BlockSpec((1, n_y, part, hidden), lambda i, p, y: (p[i], 0, 0, 0))
    made = pl.pallas_call(
        functools.partial(order_kernel, arrival(n_y), y_first),
        grid_spec=pltpu.PrefetchScalarGridSpec(
            num_scalar_prefetch=2,
            grid=(n_z,),
            in_specs=[
                spec,
                spec,
                pl.BlockSpec((hidden, n_y * part), lambda i, p, y: (0, p[i])),
            ],
            out_specs=[o[0] for o in outs],
            scratch_shapes=[pltpu.VMEM((n_y, part, hidden), BF16)],
        ),
        out_shape=[o[1] for o in outs],
        cost_estimate=pl.CostEstimate(
            flops=0, bytes_accessed=12 * width * hidden, transcendentals=0
        ),
    )(
        places,
        y[None],
        wg.reshape(n_z, n_y, part, hidden),
        wu.reshape(n_z, n_y, part, hidden),
        wd,
    )
    return [o.reshape(width, -1) for o in made]


def batched(a, b, da, db):
    return lax.dot_general(a, b, (((da,), (db,)), ((0,), (0,))), preferred_element_type=F32)


def body(saved, top_grad, norm_gain, w_gate, w_up, w_down, routes, gates):
    n_z, n_y = lax.axis_size(PIPE[0]), lax.axis_size(PIPE[1])
    n_experts = lax.axis_size("expert")
    micro, tok, part = saved.shape
    width = part * n_z * n_y
    hidden = w_gate.shape[2]
    cap = 3 * tok // n_experts
    rows = n_experts * cap
    me = lax.axis_index("expert").astype(F32)
    gain = norm_gain[:, None]
    x_t = jnp.swapaxes(saved, 1, 2)
    dy_t = jnp.swapaxes(top_grad, 1, 2)
    own_x = x_t.astype(F32)

    names = jnp.swapaxes(routes, 1, 2)
    ids = jnp.arange(n_experts, dtype=jnp.int32)
    hits = (names[:, :, None, :] == ids[None, None, :, None]).astype(F32)
    count = jnp.sum(hits, axis=1)
    lane = jnp.arange(tok, dtype=jnp.int32)
    earlier = (lane[:, None] < lane[None, :]).astype(BF16)
    before = contract(
        count.astype(BF16).reshape(micro * n_experts, tok), earlier, 1, 0
    ).reshape(micro, 1, n_experts, tok)
    slots = jnp.sum(hits * before, axis=2)
    weights = jnp.swapaxes(gates, 1, 2)
    facts = jnp.concatenate(
        [names.astype(BF16), slots.astype(BF16)] + thirds(weights) + [jnp.zeros((micro, 6, tok), BF16)],
        axis=1,
    )
    everyone = expert_gather(jnp.concatenate([x_t, dy_t, facts], axis=1))

    column = jnp.arange(n_experts * tok, dtype=jnp.int32)[None, None, :]
    first_row = (column // tok * cap).astype(F32)
    row = jnp.arange(rows, dtype=jnp.int32)[None, :, None].astype(F32)
    fact = everyone[:, 2 * part :].astype(F32)
    own = [fact[:, k : k + 1] == me for k in range(2)]
    at = [jnp.where(own[k], first_row + fact[:, 2 + k : 3 + k], -1.0) for k in range(2)]
    placing = ((row == at[0]) | (row == at[1])).astype(BF16)
    pieces = jnp.concatenate(
        [
            jnp.where(own[0], fact[:, 4 + 2 * k : 5 + 2 * k], 0.0)
            + jnp.where(own[1], fact[:, 5 + 2 * k : 6 + 2 * k], 0.0)
            for k in range(3)
        ],
        axis=1,
    ).astype(BF16)
    taken = batched(everyone[:, : 2 * part], placing, 2, 2)
    x_rows = taken[:, :part]
    saved_rows = x_rows.astype(BF16)
    blocks = jnp.concatenate(
        [(x_rows * gain).astype(BF16), taken[:, part:].astype(BF16)], axis=2
    )
    gate_rows = jnp.sum(batched(pieces, placing, 2, 2), axis=1, keepdims=True)

    line_a = gather_ring(blocks[0], PIPE[1])
    line_b = gather_ring(blocks[1], PIPE[0])
    squares = jnp.concatenate(
        [jnp.sum(x_rows * x_rows, axis=1), jnp.sum(own_x * own_x, axis=1)], axis=1
    )
    place = (lax.axis_index(PIPE[0]), lax.axis_index(PIPE[1]))
    line_a, line_b, squares, place = lax.optimization_barrier((line_a, line_b, squares, place))
    weights = (w_gate[0], w_up[0], w_down[0], n_z, n_y)

    def multiplied(sums, w, at, pieces):
        pre, back = sums
        for x in pieces:
            end = at + x.shape[0]
            p = contract(w[0][at:end], x[:, :rows], 0, 0)
            d = contract(w[1][at:end], x[:, rows:], 0, 0)
            pre = p if pre is None else pre + p
            back = d if back is None else back + d
            at = end
        return pre, back

    span_a, span_b = n_y * part, n_z * part
    ahead_b, behind_b = hop(line_b, line_b, PIPE[1])
    ahead, behind, pieces, at = line_a, line_a, [line_a], 0
    sums_a = sums_b = (None, None)
    moves = [(PIPE[1], 2), (PIPE[1], 1), (PIPE[0], 4), (PIPE[0], 2), (PIPE[0], 1)]
    w_a = w_b = None
    for s in range(1, n_z // 2):
        ahead, behind = hop(ahead, behind, PIPE[0])
        if s == 1:
            w_a = ordered_weights(place, *weights, False)
        elif s == 2:
            w_b = ordered_weights(place, *weights, True)
        else:
            sums_b = multiplied(sums_b, w_b, 0, [line_b])
        sums_a = multiplied(sums_a, w_a, at, pieces)
        at += sum(x.shape[0] for x in pieces)
        squares = add_from(*moves[2 * s - 2 : 2 * s])(squares)
        ahead, behind, place, w_a, w_b, sums_a, sums_b, squares = lax.optimization_barrier(
            (ahead, behind, place, w_a, w_b, sums_a, sums_b, squares)
        )
        pieces = [ahead, behind]
    far_a = last_hop(ahead, behind, PIPE[0])
    far_b = last_hop(ahead_b, behind_b, PIPE[1])
    sums_a = multiplied(sums_a, w_a, at, pieces + far_a)
    sums_b = multiplied(sums_b, w_b, span_b, [ahead_b, behind_b] + far_b)
    in_a, in_b = w_a[0], w_b[0]
    scale = lax.rsqrt(squares / width + EPS)[:, None, :]
    scale_rows, scale = scale[:, :, :rows], scale[:, :, rows:]

    def activations(m, pre, back):
        pre_a, pre_b = pre[:hidden] * scale_rows[m], pre[hidden:] * scale_rows[m]
        back = back * gate_rows[m]
        sig = jax.nn.sigmoid(pre_a)
        d_a = back * pre_b * sig * (1.0 + pre_a * (1.0 - sig))
        d_b = back * pre_a * sig
        inner = jnp.sum(d_a * pre[:hidden] + d_b * pre[hidden:], axis=0, keepdims=True)
        return jnp.concatenate([d_a, d_b], axis=0).astype(BF16), inner

    def terms(w_in, d, span, n):
        order = arrival(n)

        def term(off, lo, hi):
            at = order.index(off) * span
            return contract(w_in[at + lo : at + hi], d, 1, 0)

        return term

    def parts(x, n):
        order = arrival(n)

        def term(off, lo, hi):
            at = order.index(off) * part
            return x[at + lo : at + hi]

        return term

    d_b, inner_b = activations(1, *sums_b)
    d_a, inner_a = activations(0, *sums_a)
    inner = jnp.concatenate([inner_a, inner_b], axis=0)
    steps = [(PIPE[1], 2), (PIPE[1], 1), (PIPE[0], 4), (PIPE[0], 2), (PIPE[0], 1)]
    near_b, _ = scatter_ring(terms(in_b, d_b, span_b, n_y), span_b, PIPE[1])
    near_a, inner = scatter_ring(
        terms(in_a, d_a, span_a, n_z), span_a, PIPE[0], inner, steps[:4]
    )
    rows_a, inner = scatter_ring(parts(near_a, n_y), part, PIPE[1], inner, steps[4:])
    rows_b, _ = scatter_ring(parts(near_b, n_z), part, PIPE[0])
    d_rows = jnp.stack([rows_a, rows_b]).astype(BF16)

    inner = jnp.stack(thirds(inner), axis=1)
    inner = jnp.sum(batched(inner, placing, 2, 1), axis=1, keepdims=True)
    gain_part = jnp.sum(
        d_rows.astype(F32) * saved_rows.astype(F32) * scale_rows, axis=(0, 2)
    )
    gain_part = jnp.concatenate([gain_part, jnp.zeros((micro * tok - part,), F32)])
    gain_part = jnp.tile(gain_part.reshape(micro, 1, tok), (1, 1, n_experts))
    d_norm, (inner, gain_sum) = expert_return(batched(d_rows, placing, 2, 1), [inner, gain_part])
    d_x = scale * gain * d_norm - own_x * (scale * scale * scale * (inner / width))
    input_grads = jnp.swapaxes(dy_t.astype(F32) + d_x, 1, 2)
    return input_grads, gain_sum.reshape(-1)[:part]


def solution(mesh):
    torus = Mesh(mesh.devices.reshape(8, 4, mesh.shape["expert"]), (*PIPE, "expert"))
    in_specs = (
        P(None, "expert", PIPE),
        P(None, "expert", PIPE),
        P(PIPE),
        P("expert", None, PIPE),
        P("expert", None, PIPE),
        P("expert", PIPE, None),
        P(None, "expert", None),
        P(None, "expert", None),
    )
    out_specs = (P(None, "expert", PIPE), P(PIPE))
    return jax.shard_map(body, mesh=torus, in_specs=in_specs, out_specs=out_specs, check_vma=False)
```

```python
import functools

import jax
import jax.numpy as jnp
from jax import lax
from jax.experimental import pallas as pl
from jax.experimental.pallas import tpu as pltpu
from jax.sharding import Mesh
from jax.sharding import PartitionSpec as P

PIPE = ("pipe_0", "pipe_1")
EPS = 1e-05
F32 = jnp.float32
BF16 = jnp.bfloat16


def send(x, axis, to):
    n = lax.axis_size(axis)
    return lax.ppermute(x, axis, [(i, to(i) % n) for i in range(n)])


def from_offset(x, axis, d):
    return send(x, axis, lambda i: i - d)


def arrival(n):
    out = [0]
    for s in range(1, n // 2):
        out += [s, n - s]
    return out + [n // 2]


def hop(ahead, behind, axis):
    return from_offset(ahead, axis, 1), from_offset(behind, axis, -1)


def last_hop(ahead, behind, axis):
    half = ahead.shape[0] // 2
    return [from_offset(ahead[:half], axis, 1), from_offset(behind[half:], axis, -1)]


def gather_ring(x, axis):
    ahead, behind, out = x, x, [x]
    for _ in range(1, lax.axis_size(axis) // 2):
        ahead, behind = hop(ahead, behind, axis)
        out += [ahead, behind]
    return jnp.concatenate(out + last_hop(ahead, behind, axis), axis=0)


def add_from(*places):
    def step(x):
        for axis, d in places:
            x = x + from_offset(x, axis, d)
        return x

    return step


def scatter_ring(term, rows, axis, beside=None, steps=()):
    n = lax.axis_size(axis)
    half, far = rows // 2, n // 2
    up = term(far, 0, half).astype(BF16)
    down = term(far, half, rows).astype(BF16)
    steps = list(steps)
    for s in range(far - 1, -1, -1):
        got_up = from_offset(up, axis, -1)
        got_down = from_offset(down, axis, 1)
        if steps:
            other, d = steps.pop(0)
            got_up, got_down, beside = lax.optimization_barrier((got_up, got_down, beside))
            beside = beside + from_offset(beside, other, d)
        if s == far - 1:
            got_up = jnp.pad(got_up, ((0, rows - half), (0, 0)))
            got_down = jnp.pad(got_down, ((half, 0), (0, 0)))
        if s > 0:
            up = (term(s, 0, rows) + got_up.astype(F32)).astype(BF16)
            down = (term(n - s, 0, rows) + got_down.astype(F32)).astype(BF16)
    return term(0, 0, rows) + got_up.astype(F32) + got_down.astype(F32), beside


def thirds(x):
    high = lax.reduce_precision(x, 8, 7)
    rest = x - high
    middle = lax.reduce_precision(rest, 8, 7)
    return [high.astype(BF16), middle.astype(BF16), (rest - middle).astype(BF16)]


def expert_gather(x, carry=None, steps=None):
    def beside(got, k):
        nonlocal carry
        if steps is not None:
            *got, carry = lax.optimization_barrier((*got, steps[k](carry)))
        return got

    half = x.shape[0] // 2
    behind, ahead = beside(
        (send(x, "expert", lambda i: i + 2), send(x, "expert", lambda i: i - 2)), 0
    )
    one, two = beside(
        (send(behind[:half], "expert", lambda i: i + 2), send(ahead[half:], "expert", lambda i: i - 2)),
        1,
    )
    mine = jnp.concatenate([x, behind, ahead, jnp.concatenate([one, two], axis=0)], axis=2)
    (other,) = beside((send(mine, "expert", lambda i: i ^ 1),), 2)
    return jnp.concatenate([mine, other], axis=2), carry


def expert_return(x, extras):
    def packed(x, extras):
        rows = [p for e in extras for p in thirds(e)]
        pad = jnp.zeros((x.shape[0], 8 - len(rows), x.shape[2]), BF16)
        return jnp.concatenate([x.astype(BF16)] + rows + [pad], axis=1)

    def rows_of(x):
        r = x.shape[1] - 8
        return x[:, :r].astype(F32), [
            jnp.sum(x[:, r + 3 * k : r + 3 * k + 3].astype(F32), axis=1, keepdims=True)
            for k in range(len(extras))
        ]

    def plus(a, b):
        return a[0] + b[0], [p + q for p, q in zip(a[1], b[1])]

    all_ = packed(x, extras)
    block = x.shape[2] // 8
    other = send(all_[:, :, 4 * block :], "expert", lambda i: i ^ 1)
    mine = plus(rows_of(all_[:, :, : 4 * block]), rows_of(other))
    mine = packed(*mine)
    behind = rows_of(send(mine[:, :, block : 2 * block], "expert", lambda i: i - 2))
    ahead = rows_of(send(mine[:, :, 2 * block : 3 * block], "expert", lambda i: i + 2))
    far = rows_of(send(mine[:, :, 3 * block :], "expert", lambda i: i + 4))
    return plus(plus(rows_of(mine[:, :, :block]), far), plus(behind, ahead))


def contract(a, b, da, db):
    return lax.dot_general(a, b, (((da,), (db,)), ((), ())), preferred_element_type=F32)


def order_kernel(order, y_first, places, y, wg, wu, wd, into, down, turned):
    n_y, part, hidden = wg.shape[1:]
    turned[...] = wd[...].T.reshape(n_y, part, hidden)
    for j, dy in enumerate(order):
        at = lax.rem(y[0] + dy, n_y)
        to = (j, 0) if y_first else (0, j)
        into[*to, :, :hidden] = wg[0, at]
        into[*to, :, hidden:] = wu[0, at]
        down[*to] = turned[at]


def ordered_weights(place, wg, wu, wd, n_z, n_y, y_first):
    z, y = place
    width, hidden = wg.shape
    part = width // (n_z * n_y)
    places = lax.rem(z + jnp.array(arrival(n_z), jnp.int32), n_z)

    def out(cols):
        if y_first:
            return (
                pl.BlockSpec((n_y, 1, part, cols), lambda i, p, y: (0, i, 0, 0)),
                jax.ShapeDtypeStruct((n_y, n_z, part, cols), BF16),
            )
        return (
            pl.BlockSpec((1, n_y, part, cols), lambda i, p, y: (i, 0, 0, 0)),
            jax.ShapeDtypeStruct((n_z, n_y, part, cols), BF16),
        )

    outs = [out(2 * hidden), out(hidden)]
    spec = pl.BlockSpec((1, n_y, part, hidden), lambda i, p, y: (p[i], 0, 0, 0))
    made = pl.pallas_call(
        functools.partial(order_kernel, arrival(n_y), y_first),
        grid_spec=pltpu.PrefetchScalarGridSpec(
            num_scalar_prefetch=2,
            grid=(n_z,),
            in_specs=[
                spec,
                spec,
                pl.BlockSpec((hidden, n_y * part), lambda i, p, y: (0, p[i])),
            ],
            out_specs=[o[0] for o in outs],
            scratch_shapes=[pltpu.VMEM((n_y, part, hidden), BF16)],
        ),
        out_shape=[o[1] for o in outs],
        cost_estimate=pl.CostEstimate(
            flops=0, bytes_accessed=12 * width * hidden, transcendentals=0
        ),
    )(
        places,
        y[None],
        wg.reshape(n_z, n_y, part, hidden),
        wu.reshape(n_z, n_y, part, hidden),
        wd,
    )
    return [o.reshape(width, -1) for o in made]


def batched(a, b, da, db):
    return lax.dot_general(a, b, (((da,), (db,)), ((0,), (0,))), preferred_element_type=F32)


def body(saved, top_grad, norm_gain, w_gate, w_up, w_down, routes, gates):
    n_z, n_y = lax.axis_size(PIPE[0]), lax.axis_size(PIPE[1])
    n_experts = lax.axis_size("expert")
    micro, tok, part = saved.shape
    width = part * n_z * n_y
    hidden = w_gate.shape[2]
    cap = 3 * tok // n_experts
    rows = n_experts * cap
    me = lax.axis_index("expert").astype(F32)
    gain = norm_gain[:, None]
    x_t = jnp.swapaxes(saved, 1, 2)
    dy_t = jnp.swapaxes(top_grad, 1, 2)
    own_x = x_t.astype(F32)

    moves = [(PIPE[1], 2), (PIPE[1], 1), (PIPE[0], 4), (PIPE[0], 2), (PIPE[0], 1)]
    squares = jnp.sum(own_x * own_x, axis=1, keepdims=True)

    names = jnp.swapaxes(routes, 1, 2)
    ids = jnp.arange(n_experts, dtype=jnp.int32)
    hits = (names[:, :, None, :] == ids[None, None, :, None]).astype(F32)
    count = jnp.sum(hits, axis=1)
    lane = jnp.arange(tok, dtype=jnp.int32)
    earlier = (lane[:, None] < lane[None, :]).astype(BF16)
    before = contract(
        count.astype(BF16).reshape(micro * n_experts, tok), earlier, 1, 0
    ).reshape(micro, 1, n_experts, tok)
    slots = jnp.sum(hits * before, axis=2)
    weights = jnp.swapaxes(gates, 1, 2)
    facts = jnp.concatenate(
        [names.astype(BF16), slots.astype(BF16)] + thirds(weights) + [jnp.zeros((micro, 6, tok), BF16)],
        axis=1,
    )
    everyone, squares = expert_gather(
        jnp.concatenate([x_t, dy_t, facts], axis=1),
        squares,
        [add_from(*moves[:2]), add_from(*moves[2:4]), add_from(*moves[4:])],
    )

    column = jnp.arange(n_experts * tok, dtype=jnp.int32)[None, None, :]
    first_row = (column // tok * cap).astype(F32)
    row = jnp.arange(rows, dtype=jnp.int32)[None, :, None].astype(F32)
    fact = everyone[:, 2 * part :].astype(F32)
    own = [fact[:, k : k + 1] == me for k in range(2)]
    at = [jnp.where(own[k], first_row + fact[:, 2 + k : 3 + k], -1.0) for k in range(2)]
    placing = ((row == at[0]) | (row == at[1])).astype(BF16)
    pieces = jnp.concatenate(
        [
            jnp.where(own[0], fact[:, 4 + 2 * k : 5 + 2 * k], 0.0)
            + jnp.where(own[1], fact[:, 5 + 2 * k : 6 + 2 * k], 0.0)
            for k in range(3)
        ],
        axis=1,
    ).astype(BF16)
    taken = batched(everyone[:, : 2 * part], placing, 2, 2)
    x_rows = taken[:, :part]
    saved_rows = x_rows.astype(BF16)
    blocks = jnp.concatenate(
        [(x_rows * gain).astype(BF16), taken[:, part:].astype(BF16)], axis=2
    )
    gate_rows = jnp.sum(batched(pieces, placing, 2, 2), axis=1, keepdims=True)

    scale = lax.rsqrt(squares / width + EPS)
    scale_parts = jnp.concatenate(thirds(scale) + [jnp.zeros((micro, 5, tok), BF16)], axis=1)
    line_a = gather_ring(blocks[0], PIPE[1])
    line_b = gather_ring(blocks[1], PIPE[0])
    place = (lax.axis_index(PIPE[0]), lax.axis_index(PIPE[1]))
    line_a, line_b, place = lax.optimization_barrier((line_a, line_b, place))
    weights = (w_gate[0], w_up[0], w_down[0], n_z, n_y)

    def multiplied(sums, w, at, pieces):
        pre, back = sums
        for x in pieces:
            end = at + x.shape[0]
            p = contract(w[0][at:end], x[:, :rows], 0, 0)
            d = contract(w[1][at:end], x[:, rows:], 0, 0)
            pre = p if pre is None else pre + p
            back = d if back is None else back + d
            at = end
        return pre, back

    span_a, span_b = n_y * part, n_z * part
    ahead_b, behind_b = hop(line_b, line_b, PIPE[1])
    ahead, behind, pieces, at = line_a, line_a, [line_a], 0
    sums_a = sums_b = (None, None)
    w_a = w_b = None
    for s in range(1, n_z // 2):
        ahead, behind = hop(ahead, behind, PIPE[0])
        if s == 1:
            w_a = ordered_weights(place, *weights, False)
        elif s == 2:
            w_b = ordered_weights(place, *weights, True)
        else:
            sums_b = multiplied(sums_b, w_b, 0, [line_b])
            scale_parts, _ = expert_gather(scale_parts)
        sums_a = multiplied(sums_a, w_a, at, pieces)
        at += sum(x.shape[0] for x in pieces)
        ahead, behind, place, w_a, w_b, sums_a, sums_b, scale_parts = lax.optimization_barrier(
            (ahead, behind, place, w_a, w_b, sums_a, sums_b, scale_parts)
        )
        pieces = [ahead, behind]
    far_a = last_hop(ahead, behind, PIPE[0])
    far_b = last_hop(ahead_b, behind_b, PIPE[1])
    sums_a = multiplied(sums_a, w_a, at, pieces + far_a)
    sums_b = multiplied(sums_b, w_b, span_b, [ahead_b, behind_b] + far_b)
    in_a, in_b = w_a[0], w_b[0]
    scale_rows = jnp.sum(batched(scale_parts, placing, 2, 2), axis=1, keepdims=True)

    def activations(m, pre, back):
        pre_a, pre_b = pre[:hidden] * scale_rows[m], pre[hidden:] * scale_rows[m]
        back = back * gate_rows[m]
        sig = jax.nn.sigmoid(pre_a)
        d_a = back * pre_b * sig * (1.0 + pre_a * (1.0 - sig))
        d_b = back * pre_a * sig
        inner = jnp.sum(d_a * pre[:hidden] + d_b * pre[hidden:], axis=0, keepdims=True)
        return jnp.concatenate([d_a, d_b], axis=0).astype(BF16), inner

    def terms(w_in, d, span, n):
        order = arrival(n)

        def term(off, lo, hi):
            at = order.index(off) * span
            return contract(w_in[at + lo : at + hi], d, 1, 0)

        return term

    def parts(x, n):
        order = arrival(n)

        def term(off, lo, hi):
            at = order.index(off) * part
            return x[at + lo : at + hi]

        return term

    d_b, inner_b = activations(1, *sums_b)
    d_a, inner_a = activations(0, *sums_a)
    inner = jnp.concatenate([inner_a, inner_b], axis=0)
    steps = moves[2:] + moves[:2]
    near_b, _ = scatter_ring(terms(in_b, d_b, span_b, n_y), span_b, PIPE[1])
    near_a, inner = scatter_ring(
        terms(in_a, d_a, span_a, n_z), span_a, PIPE[0], inner, steps[:4]
    )
    rows_a, inner = scatter_ring(parts(near_a, n_y), part, PIPE[1], inner, steps[4:])
    rows_b, _ = scatter_ring(parts(near_b, n_z), part, PIPE[0])
    d_rows = jnp.stack([rows_a, rows_b]).astype(BF16)

    inner = jnp.stack(thirds(inner), axis=1)
    inner = jnp.sum(batched(inner, placing, 2, 1), axis=1, keepdims=True)
    gain_part = jnp.sum(
        d_rows.astype(F32) * saved_rows.astype(F32) * scale_rows, axis=(0, 2)
    )
    gain_part = jnp.concatenate([gain_part, jnp.zeros((micro * tok - part,), F32)])
    gain_part = jnp.tile(gain_part.reshape(micro, 1, tok), (1, 1, n_experts))
    d_norm, (inner, gain_sum) = expert_return(batched(d_rows, placing, 2, 1), [inner, gain_part])
    d_x = scale * gain * d_norm - own_x * (scale * scale * scale * (inner / width))
    input_grads = jnp.swapaxes(dy_t.astype(F32) + d_x, 1, 2)
    return input_grads, gain_sum.reshape(-1)[:part]


def solution(mesh):
    torus = Mesh(mesh.devices.reshape(8, 4, mesh.shape["expert"]), (*PIPE, "expert"))
    in_specs = (
        P(None, "expert", PIPE),
        P(None, "expert", PIPE),
        P(PIPE),
        P("expert", None, PIPE),
        P("expert", None, PIPE),
        P("expert", PIPE, None),
        P(None, "expert", None),
        P(None, "expert", None),
    )
    out_specs = (P(None, "expert", PIPE), P(PIPE))
    return jax.shard_map(body, mesh=torus, in_specs=in_specs, out_specs=out_specs, check_vma=False)
```
